128 devices in a mesh: section: 2 (over core), dp: 4 (over x), mp: 16 (over z, y).
Axes of the slice: x: 4, y: 4, z: 4, core: 2. Of those that a mesh axis runs over, the one named last changes fastest.
Arguments:
- segment_input: bfloat16 [2, 4, 256, 2048], P(None, 'dp', None, 'mp'), may hold values from -6 to 6
- out_grad: bfloat16 [2, 4, 256, 2048], P(None, 'dp', None, 'mp'), may hold values from -6 to 6
- pool_tokens: bfloat16 [16, 4, 128, 896], P('section', 'dp'), may hold values from -6 to 6
- neighbour_ids: int32 [2, 4, 4, 4], P(None, 'dp'), may hold values from 0 to 15, as said below
- neighbour_counts: int32 [2, 4, 4], P(None, 'dp'), may hold values from 1 to 4
- enc_gain: float32 [896], replicated, may hold values from 0.5 to 1.5
- enc_up: bfloat16 [896, 4096], P(None, 'mp'), may hold values from -0.1875 to 0.1875
- enc_down: bfloat16 [4096, 896], P(None, 'mp'), may hold values from -0.09375 to 0.09375
- norm_gain: float32 [2, 2048], P('section'), may hold values from 0.5 to 1.5
- w_query: bfloat16 [2, 2048, 4096], P('section', None, 'mp'), may hold values from -0.125 to 0.125
- w_key: bfloat16 [2, 896, 4096], P('section', None, 'mp'), may hold values from -0.1875 to 0.1875
- w_value: bfloat16 [2, 896, 4096], P('section', None, 'mp'), may hold values from -0.1875 to 0.1875
- w_out: bfloat16 [2, 4096, 2048], P('section', None, 'mp'), may hold values from -0.09375 to 0.09375
Outputs:
- grad_key: bfloat16 [2, 896, 4096], P('section', None, 'mp')
- grad_value: bfloat16 [2, 896, 4096], P('section', None, 'mp')
The draws below stay inside these ranges and needn't reach their ends.
Inputs may be any that keep to these rules, and one draw needn't show every extreme that they name: `neighbour_ids`: the 4 slots of one stretch name distinct pool stretches.
All inputs are finite; a program needn't handle non-finite values.
Results may differ from the reference program's by a relative error of at most 0.025.
Values may be sent and summed in bfloat16 or wider, within the bound.
A program may use at most 128 MiB of HBM per device.

```python
import jax
import jax.numpy as jnp
from jax import lax

D = 2048
HEAD = 128
ENC = 896
STRETCH = 64
NT = 128
KMAX = 4
MB = 2
CPM = 4
HEADS = 32
HQ = 4096
ENC_FF = 4096
RM = 256
POOL = 16
GROUPS = 4
SECTIONS = 2
N_MP = 16


def draw_neighbour_counts(key, part):
    base = jax.random.randint(jax.random.fold_in(key, 11), (MB * GROUPS * CPM,), 1, KMAX + 1)
    total_count = MB * GROUPS * CPM
    full_place = jax.random.randint(jax.random.fold_in(key, 12), (), 0, total_count)
    low_place = (full_place + 1) % total_count
    positions = jnp.arange(total_count)
    base = jnp.where(positions == full_place, KMAX, base)
    base = jnp.where(positions == low_place, 1, base)
    return base.reshape(MB, GROUPS, CPM).astype(jnp.int32)


def draw_neighbour_ids(key, part):
    total_count = MB * GROUPS * CPM
    row_keys = jax.random.split(jax.random.fold_in(key, 21), total_count)
    picks = jax.vmap(lambda row_key: jax.random.permutation(row_key, POOL)[:KMAX])(row_keys)
    top_place = jax.random.randint(jax.random.fold_in(key, 22), (), 0, total_count)
    bottom_place = (top_place + 1) % total_count
    positions = jnp.arange(total_count)[:, None]
    slot_index = jnp.arange(KMAX)[None, :]
    picks = jnp.where(positions == top_place, POOL - 1 - slot_index, picks)
    picks = jnp.where(positions == bottom_place, slot_index, picks)
    return picks.reshape(MB, GROUPS, CPM, KMAX).astype(jnp.int32)


def level_of(stream_key, shape, pieces, low, high):
    def one(dim, shards_of):
        draws = jax.random.uniform(jax.random.fold_in(jax.random.fold_in(stream_key, 6), dim), (shards_of,), jnp.float32, low / len(pieces), high / len(pieces))
        return jnp.repeat(jnp.exp(draws), shape[dim] // shards_of).reshape((-1,) + (1,) * (len(shape) - dim - 1))

    loudness = one(*pieces[0])
    for cut in pieces[1:]:
        loudness = loudness * one(*cut)
    return loudness


def scatter_about(stream_key, shape, spread, most, cuts=(), kind=jnp.bfloat16):
    entries = spread * jax.random.normal(stream_key, shape, jnp.float32)
    if cuts:
        entries = entries * level_of(stream_key, shape, cuts, -0.22, 0.18)
    return jnp.clip(entries, -most, most).astype(kind)


def setup_inputs(seed: int = 0) -> dict:
    splits = jax.random.split(jax.random.key(seed), 14)
    return {
        "segment_input": scatter_about(splits[0], (MB, GROUPS, RM, D), 1.0, 6.0, ((1, 4), (3, 16))),
        "out_grad": scatter_about(splits[1], (MB, GROUPS, RM, D), 1.0, 6.0, ((1, 4), (3, 16))),
        "pool_tokens": scatter_about(splits[2], (POOL, GROUPS, NT, ENC), 1.0, 6.0, ((0, 2), (1, 4))),
        "neighbour_ids": draw_neighbour_ids(jax.random.fold_in(splits[13], 71), 0),
        "neighbour_counts": draw_neighbour_counts(jax.random.fold_in(splits[13], 71), 0),
        "enc_gain": jnp.clip(1.0 + 0.1 * jax.random.normal(splits[5], (ENC,), jnp.float32), 0.5, 1.5),
        "enc_up": scatter_about(splits[6], (ENC, ENC_FF), ENC ** -0.5, 0.1875, ((1, 16),)),
        "enc_down": scatter_about(splits[7], (ENC_FF, ENC), ENC_FF ** -0.5, 0.09375, ((1, 16),)),
        "norm_gain": jnp.clip(1.0 + 0.1 * jax.random.normal(splits[8], (SECTIONS, D), jnp.float32), 0.5, 1.5),
        "w_query": scatter_about(splits[9], (SECTIONS, D, HQ), D ** -0.5, 0.125, ((0, 2), (2, 16))),
        "w_key": scatter_about(splits[10], (SECTIONS, ENC, HQ), ENC ** -0.5, 0.1875, ((0, 2), (2, 16))),
        "w_value": scatter_about(splits[11], (SECTIONS, ENC, HQ), ENC ** -0.5, 0.1875, ((0, 2), (2, 16))),
        "w_out": scatter_about(splits[12], (SECTIONS, HQ, D), HQ ** -0.5, 0.09375, ((0, 2), (2, 16))),
    }


EPSILON = 1e-05

def to_bf16(values):
    return lax.optimization_barrier(values.astype(jnp.bfloat16))

def rms_scale(values):
    return lax.rsqrt(lax.optimization_barrier(jnp.mean(values * values, axis=-1, keepdims=True)) + EPSILON)

def encode_pool(raw_rows, enc_gain, enc_up, enc_down):
    raw_wide = raw_rows.astype(jnp.float32)
    normed = to_bf16(raw_wide * rms_scale(raw_wide) * enc_gain)
    hidden = to_bf16(jax.nn.gelu(jnp.dot(normed, enc_up, preferred_element_type=jnp.float32)))
    return (raw_wide + jnp.dot(hidden, enc_down, preferred_element_type=jnp.float32)).astype(jnp.bfloat16)

def attend(queries, key_block, value_block, usable):
    scores = jnp.einsum('cqhe,ckhe->chqk', queries.astype(jnp.float32), key_block.astype(jnp.float32))
    scores = jnp.where(usable[:, None, None, :], scores, -1e+30)
    weights = jax.nn.softmax(scores, axis=-1)
    weights_bf = to_bf16(weights)
    attended = jnp.einsum('chqk,ckhe->cqhe', weights_bf.astype(jnp.float32), value_block.astype(jnp.float32))
    return (weights, weights_bf, attended.astype(jnp.bfloat16))

def attend_back(queries, key_block, value_block, weights, weights_bf, grad_attended):
    grad_wide = grad_attended.astype(jnp.float32)
    grad_weights = jnp.einsum('cqhe,ckhe->chqk', grad_wide, value_block.astype(jnp.float32))
    grad_scores = weights * (grad_weights - lax.optimization_barrier(jnp.sum(weights * grad_weights, axis=-1, keepdims=True)))
    grad_values = jnp.einsum('chqk,cqhe->ckhe', weights_bf.astype(jnp.float32), grad_wide).astype(jnp.bfloat16)
    grad_keys = jnp.einsum('chqk,cqhe->ckhe', grad_scores, queries.astype(jnp.float32)).astype(jnp.bfloat16)
    grad_queries = jnp.einsum('chqk,ckhe->cqhe', grad_scores, key_block.astype(jnp.float32))
    return (grad_keys, grad_values, grad_queries)

def reference(segment_input, out_grad, pool_tokens, neighbour_ids, neighbour_counts, enc_gain, enc_up, enc_down, norm_gain, w_query, w_key, w_value, w_out):
    head_scale = HEAD ** (-0.5)
    key_span = KMAX * NT
    segment_params = (norm_gain, w_query, w_key, w_value, w_out)
    contract = (((0,), (0,)), ((), ()))

    def front(rows_in, gain, query_w, key_block, value_block, usable):
        rows_wide = rows_in.astype(jnp.float32)
        inv_rms = rms_scale(rows_wide)
        normed = to_bf16(rows_wide * inv_rms * gain)
        query_raw = jnp.dot(normed, query_w, preferred_element_type=jnp.float32)
        queries = to_bf16(query_raw * head_scale).reshape(CPM, STRETCH, HEADS, HEAD)
        weights, weights_bf, attended = attend(queries, key_block, value_block, usable)
        return (inv_rms, query_raw, queries, weights, weights_bf, attended)

    def one_group(totals, group_data):
        inputs_g, grads_g, raw_g, ids_g, counts_g = group_data
        encoded = encode_pool(raw_g.reshape(POOL * NT, ENC), enc_gain, enc_up, enc_down).reshape(POOL, NT, ENC)
        sum_keys, sum_values = totals
        for micro_index in range(MB):
            neighbours = encoded[ids_g[micro_index]].reshape(CPM * key_span, ENC)
            usable = (jnp.arange(key_span, dtype=jnp.int32) // NT)[None, :] < counts_g[micro_index][:, None]

            def project(weight):
                projected = jnp.dot(neighbours, weight, preferred_element_type=jnp.float32).astype(jnp.bfloat16)
                return projected.reshape(CPM, key_span, HEADS, HEAD)

            def forward(rows_in, params):
                gain, query_w, key_w, value_w, out_w = params
                outputs = front(rows_in, gain, query_w, project(key_w), project(value_w), usable)
                attended = outputs[5].reshape(CPM * STRETCH, HQ)
                result = rows_in.astype(jnp.float32) + jnp.dot(attended, out_w, preferred_element_type=jnp.float32)
                return (result.astype(jnp.bfloat16), rows_in)
            _, saved = lax.scan(forward, inputs_g[micro_index], segment_params)

            def backward(grad_rows, packed):
                rows_in, gain, query_w, key_w, value_w, out_w = packed
                key_block = project(key_w)
                value_block = project(value_w)
                inv_rms, query_raw, queries, weights, weights_bf, _ = front(rows_in, gain, query_w, key_block, value_block, usable)
                grad_att = to_bf16(jnp.dot(grad_rows, out_w.T, preferred_element_type=jnp.float32)).reshape(CPM, STRETCH, HEADS, HEAD)
                grad_keys, grad_values, grad_queries = attend_back(queries, key_block, value_block, weights, weights_bf, grad_att)
                grad_scaled = to_bf16((grad_queries * head_scale).reshape(CPM * STRETCH, HQ))
                part_totals = lax.optimization_barrier(jnp.sum((grad_scaled.astype(jnp.float32) * query_raw).reshape(CPM * STRETCH, N_MP, HQ // N_MP), axis=2))
                row_total = lax.optimization_barrier(jnp.sum(to_bf16(part_totals).astype(jnp.float32), axis=1, keepdims=True))
                grad_normed = jnp.dot(grad_scaled, query_w.T, preferred_element_type=jnp.float32)
                rows_wide = rows_in.astype(jnp.float32)
                grad_in = grad_rows.astype(jnp.float32) + inv_rms * gain * grad_normed - rows_wide * inv_rms * inv_rms * row_total / D
                key_grad = lax.dot_general(neighbours, grad_keys.reshape(CPM * key_span, HQ), contract, preferred_element_type=jnp.float32)
                value_grad = lax.dot_general(neighbours, grad_values.reshape(CPM * key_span, HQ), contract, preferred_element_type=jnp.float32)
                return (grad_in.astype(jnp.bfloat16), (key_grad, value_grad))
            _, (key_grads, value_grads) = lax.scan(backward, grads_g[micro_index], (saved,) + segment_params, reverse=True)
            sum_keys = sum_keys + key_grads
            sum_values = sum_values + value_grads
        return ((sum_keys, sum_values), None)
    group_data = (jnp.moveaxis(segment_input, 1, 0), jnp.moveaxis(out_grad, 1, 0), jnp.moveaxis(pool_tokens, 1, 0), jnp.moveaxis(neighbour_ids, 1, 0), jnp.moveaxis(neighbour_counts, 1, 0))
    start_totals = (jnp.zeros((SECTIONS, ENC, HQ), jnp.float32), jnp.zeros((SECTIONS, ENC, HQ), jnp.float32))
    (sum_keys, sum_values), _ = lax.scan(one_group, start_totals, group_data)
    return (sum_keys.astype(jnp.bfloat16), sum_values.astype(jnp.bfloat16))
```

```python
import functools

import jax
import jax.numpy as jnp
from jax import lax
from jax.experimental import pallas as pl
from jax.experimental.pallas import tpu as pltpu
from jax.sharding import PartitionSpec as P

HEAD = 128
NT = 128
SIDE = 4
EPSILON = 1e-05
SCALE = HEAD ** (-0.5)
VMEM = pltpu.VMEM
BF = jnp.bfloat16
F32 = jnp.float32
LIMIT = 60 * 1024 * 1024

OFFSETS = [(2, 2), (2, 1), (2, 3), (1, 2), (3, 2), (1, 1), (3, 3), (1, 3), (3, 1),
           (2, 0), (0, 2), (1, 0), (0, 1), (3, 0), (0, 3)]


def dims(lhs, rhs):
    return (((lhs,), (rhs,)), ((), ()))


def mul(a, b, lhs=1, rhs=0):
    return lax.dot_general(a, b, dims(lhs, rhs), preferred_element_type=F32)


def rms_scale(values):
    return lax.rsqrt(jnp.mean(values * values, axis=-1, keepdims=True) + EPSILON)


def shifted(m, dz, dy):
    z = lax.rem(lax.div(m, SIDE) + dz, SIDE)
    y = lax.rem(lax.rem(m, SIDE) + dy, SIDE)
    return z * SIDE + y


def to_peer(m, k):
    return shifted(m, *OFFSETS[k])


def from_peer(m, k):
    dz, dy = OFFSETS[k]
    return shifted(m, (SIDE - dz) % SIDE, (SIDE - dy) % SIDE)


def remote(src, dst, send, recv, device):
    return pltpu.make_async_remote_copy(
        src_ref=src, dst_ref=dst, send_sem=send, recv_sem=recv,
        device_id=device, device_id_type=pl.DeviceIdType.MESH,
    )


def greet(devices):
    barrier = pltpu.get_barrier_semaphore()
    for device in devices:
        pl.semaphore_signal(
            barrier, inc=1, device_id=device, device_id_type=pl.DeviceIdType.MESH
        )
    pl.semaphore_wait(barrier, len(devices))


def rows_of(index, size):
    return pl.ds(pl.multiple_of(index * size, size), size)


def encode_kernel(
    x_ref, wo_ref, ed_ref, pool_ref, gain_ref, up_ref,
    enc_ref, xf_ref, wor_ref,
    edr, dt, hid, part, rs,
    own_sem, ed_s, ed_r, x_s, x_r, wo_s, wo_r, rs_s, rs_r, ag_s, ag_r, fw_s, fw_r,
):
    s = lax.axis_index("section")
    m = lax.axis_index("mp")
    other = {"section": 1 - s}
    count = len(OFFSETS)
    greet([{"mp": to_peer(m, k)} for k in range(count)] + [other])
    span = wor_ref.shape[0]
    cols = rows_of(m, HEAD)
    own = [
        pltpu.make_async_copy(x_ref, xf_ref.at[:, cols], own_sem.at[0]),
        pltpu.make_async_copy(wo_ref.at[rows_of(m, span), :], wor_ref.at[:, cols], own_sem.at[1]),
        pltpu.make_async_copy(ed_ref.at[m], edr.at[m], own_sem.at[2]),
    ]
    for copy in own:
        copy.start()
    sends = []
    for k in range(count):
        p = to_peer(m, k)
        sends.append(remote(ed_ref.at[p], edr.at[m], ed_s.at[k], ed_r.at[k], {"mp": p}))
        sends[-1].start()
    for k in range(count):
        p = to_peer(m, k)
        sends.append(remote(wo_ref.at[rows_of(p, span), :], wor_ref.at[:, cols],
                            wo_s.at[k], wo_r.at[k], {"mp": p}))
        sends[-1].start()
        sends.append(remote(x_ref, xf_ref.at[:, cols], x_s.at[k], x_r.at[k], {"mp": p}))
        sends[-1].start()

    gain = gain_ref[...]

    def hidden_rows(i, carry):
        rows = rows_of(i, 256)
        wide = pool_ref[rows, :].astype(F32)
        normed = (wide * rms_scale(wide) * gain).astype(BF)
        hid[rows, :] = jax.nn.gelu(mul(normed, up_ref[...])).astype(BF)
        return carry

    lax.fori_loop(0, SIDE, hidden_rows, 0)

    own[2].wait()
    for k in range(count):
        p = from_peer(m, k)
        remote(ed_ref.at[p], edr.at[p], ed_s.at[k], ed_r.at[k], {"mp": p}).wait_recv()
    feat = enc_ref.shape[1] // len(edr)
    for p in range(len(edr)):
        dt[pl.ds(p * feat, feat), :] = edr[p, pl.ds(0, feat), :].astype(F32)
    down = dt[...].astype(BF)
    shard = rs.shape[1]
    for dz in (2, 1, 3, 0):
        block = rows_of(lax.rem(lax.div(m, SIDE) + dz, SIDE), SIDE * shard)
        part[block, :] = mul(hid[block, :], down, 1, 1).astype(BF)
        for k in range(count):
            if OFFSETS[k][0] != dz:
                continue
            p = to_peer(m, k)
            sends.append(remote(part.at[rows_of(p, shard), :], rs.at[k],
                                rs_s.at[k], rs_r.at[k], {"mp": p}))
            sends[-1].start()
    mine = rows_of(m, shard)
    total = pool_ref[mine, :].astype(F32) + part[mine, :].astype(F32)
    for k in range(count):
        p = from_peer(m, k)
        remote(part.at[rows_of(p, shard), :], rs.at[k], rs_s.at[k], rs_r.at[k], {"mp": p}).wait_recv()
        total = total + rs[k].astype(F32)
    half = s * len(edr)
    place = rows_of(half + m, shard)
    enc_ref[place, :] = total.astype(BF)
    for k in range(count):
        p = to_peer(m, k)
        sends.append(remote(enc_ref.at[place, :], enc_ref.at[place, :],
                            ag_s.at[k], ag_r.at[k], {"mp": p}))
        sends[-1].start()
    sends.append(remote(enc_ref.at[place, :], enc_ref.at[place, :],
                        fw_s.at[count], fw_r.at[count], other))
    sends[-1].start()
    for k in reversed(range(count)):
        p = from_peer(m, k)
        there = rows_of(half + p, shard)
        remote(enc_ref.at[there, :], enc_ref.at[there, :], ag_s.at[k], ag_r.at[k], {"mp": p}).wait_recv()
        sends.append(remote(enc_ref.at[there, :], enc_ref.at[there, :],
                            fw_s.at[k], fw_r.at[k], other))
        sends[-1].start()
    away = (1 - s) * len(edr)
    for k in range(count + 1):
        p = m if k == count else from_peer(m, k)
        there = rows_of(away + p, shard)
        remote(enc_ref.at[there, :], enc_ref.at[there, :], fw_s.at[k], fw_r.at[k], other).wait_recv()
    for k in range(count):
        p = from_peer(m, k)
        there = rows_of(p, HEAD)
        remote(wo_ref.at[rows_of(p, span), :], wor_ref.at[:, there],
               wo_s.at[k], wo_r.at[k], {"mp": p}).wait_recv()
        remote(x_ref, xf_ref.at[:, there], x_s.at[k], x_r.at[k], {"mp": p}).wait_recv()
    own[0].wait()
    own[1].wait()
    for copy in sends:
        copy.wait_send()


def encode(x, wo, ed, pool, gain, up):
    peers, _, span = ed.shape
    rows, enc = pool.shape
    dma = pltpu.SemaphoreType.DMA
    count = len(OFFSETS)
    vmem = pl.BlockSpec(memory_space=VMEM)
    hbm = pl.BlockSpec(memory_space=pl.ANY)
    return pl.pallas_call(
        encode_kernel,
        name="encode_exchange",
        out_shape=(
            jax.ShapeDtypeStruct((2 * rows, enc), BF),
            jax.ShapeDtypeStruct((x.shape[0], x.shape[1] * peers), BF),
            jax.ShapeDtypeStruct((span, wo.shape[1] * peers), BF),
        ),
        in_specs=[hbm, hbm, hbm, vmem, vmem, vmem],
        out_specs=(vmem,) * 3,
        scratch_shapes=[
            VMEM(ed.shape, BF), VMEM((enc, span), F32), VMEM((rows, span), BF),
            VMEM((rows, enc), BF), VMEM((count, rows // peers, enc), BF),
            dma((3,)),
        ] + [dma((count,))] * 10 + [dma((count + 1,))] * 2,
        compiler_params=pltpu.CompilerParams(
            collective_id=0, has_side_effects=True, vmem_limit_bytes=LIMIT),
    )(x, wo, ed, pool, gain, up)


def head_cols(h):
    return pl.ds(h * HEAD, HEAD)


def gathered(ref, ids_ref, c, columns):
    slots = ids_ref.shape[1]
    return jnp.concatenate(
        [ref[rows_of(ids_ref[c, j], NT), columns] for j in range(slots)], axis=0)


def soft(scores, used):
    slot = lax.div(lax.broadcasted_iota(jnp.int32, scores.shape, 1), NT)
    scores = jnp.where(slot < used, scores, -1e30)
    grown = jnp.exp(scores - jnp.max(scores, axis=-1, keepdims=True))
    return grown / jnp.sum(grown, axis=-1, keepdims=True)


def queries_of(x_ref, gain_ref, wq_ref, q_ref):
    def some(i, carry):
        rows = rows_of(i, 256)
        wide = x_ref[rows, :].astype(F32)
        normed = (wide * rms_scale(wide) * gain_ref[...]).astype(BF)
        q_ref[rows, :] = (mul(normed, wq_ref[...]) * SCALE).astype(BF)
        return carry

    lax.fori_loop(0, x_ref.shape[0] // 256, some, 0)


def grad_attended(x_ref, wor_ref, ga_ref):
    def some(i, carry):
        rows = rows_of(i, 256)
        ga_ref[rows, :] = mul(x_ref[rows, :], wor_ref[...], 1, 1).astype(BF)
        return carry

    lax.fori_loop(0, x_ref.shape[0] // 256, some, 0)


def front_kernel(ids_ref, used_ref, x_ref, gain_ref, wq_ref, enc_ref, wk_ref, wv_ref, wor_ref,
                 k_ref, v_ref, q_ref, p_ref, part_ref, ga_ref):
    s = lax.axis_index("section")

    def project(i, carry):
        rows = rows_of(i, 512)
        block = enc_ref[rows, :]
        k_ref[rows, :] = mul(block, wk_ref[...]).astype(BF)
        v_ref[rows, :] = mul(block, wv_ref[...]).astype(BF)
        return carry

    lax.fori_loop(0, enc_ref.shape[0] // 512, project, 0)
    heads = q_ref.shape[1] // HEAD
    tracts = ids_ref.shape[0]
    size = x_ref.shape[0] // tracts

    @pl.when(s == 0)
    def _():
        queries_of(x_ref, gain_ref, wq_ref, q_ref)

        def tract(c, carry):
            rows = rows_of(c, size)
            found = []
            for h in range(heads):
                keys = gathered(k_ref, ids_ref, c, head_cols(h))
                probs = soft(mul(q_ref[rows, head_cols(h)], keys, 1, 1), used_ref[c])
                p_ref[c, h] = probs
                values = gathered(v_ref, ids_ref, c, head_cols(h))
                found.append(mul(probs.astype(BF), values).astype(BF))
            part_ref[rows, :] = mul(jnp.concatenate(found, axis=1), wor_ref[...]).astype(BF)
            return carry

        lax.fori_loop(0, tracts, tract, 0)

    @pl.when(s != 0)
    def _():
        grad_attended(x_ref, wor_ref, ga_ref)


def back_tract(c, rows, heads, ids_ref, enc_ref, k_ref, v_ref, q_ref, ga_ref, probs_of, acc_k, acc_v,
               scores_used):
    near = gathered(enc_ref, ids_ref, c, slice(None))
    key_t, value_t, query_g = [], [], []
    for h in range(heads):
        q = q_ref[rows, head_cols(h)]
        ga = ga_ref[rows, head_cols(h)]
        values = gathered(v_ref, ids_ref, c, head_cols(h))
        keys = None
        if k_ref is not None:
            keys = gathered(k_ref, ids_ref, c, head_cols(h))
        probs = probs_of(h, q, keys)
        grad_probs = mul(ga, values, 1, 1)
        grad_scores = probs * (grad_probs - jnp.sum(probs * grad_probs, axis=-1, keepdims=True))
        grad_scores = grad_scores.astype(BF)
        value_t.append(mul(ga, probs.astype(BF), 0, 0).astype(BF))
        key_t.append(mul(q, grad_scores, 0, 0).astype(BF))
        if keys is not None:
            query_g.append((mul(grad_scores, keys) * SCALE).astype(BF))
    acc_k[...] += mul(jnp.concatenate(key_t, axis=0), near)
    acc_v[...] += mul(jnp.concatenate(value_t, axis=0), near)
    return query_g


def late_kernel(ids_ref, used_ref, x_ref, gain_ref, wq_ref, enc_ref, k_ref, v_ref, ga_ref,
                part_ref, sk_ref, sv_ref, q_ref, acc_k, acc_v):
    heads = q_ref.shape[1] // HEAD
    tracts = ids_ref.shape[0]
    size = x_ref.shape[0] // tracts

    @pl.when(lax.axis_index("section") != 0)
    def _():
        queries_of(x_ref, gain_ref, wq_ref, q_ref)
        acc_k[...] = jnp.zeros_like(acc_k)
        acc_v[...] = jnp.zeros_like(acc_v)

        def tract(c, carry):
            rows = rows_of(c, size)

            def probs_of(h, q, keys):
                return soft(mul(q, keys, 1, 1), used_ref[c])

            query_g = back_tract(c, rows, heads, ids_ref, enc_ref, k_ref, v_ref, q_ref, ga_ref,
                                 probs_of, acc_k, acc_v, None)
            part_ref[rows, :] = mul(jnp.concatenate(query_g, axis=1), wq_ref[...], 1, 1).astype(BF)
            return carry

        lax.fori_loop(0, tracts, tract, 0)
        sk_ref[...] = jnp.transpose(acc_k[...]).astype(BF)
        sv_ref[...] = jnp.transpose(acc_v[...]).astype(BF)


def early_kernel(ids_ref, g_ref, wor_ref, enc_ref, v_ref, q_ref, p_ref, lk_ref, lv_ref,
                 sk_ref, sv_ref, ga_ref, acc_k, acc_v):
    heads = q_ref.shape[1] // HEAD
    tracts = ids_ref.shape[0]
    size = g_ref.shape[0] // tracts
    s = lax.axis_index("section")

    @pl.when(s == 0)
    def _():
        grad_attended(g_ref, wor_ref, ga_ref)
        acc_k[...] = jnp.zeros_like(acc_k)
        acc_v[...] = jnp.zeros_like(acc_v)

        def tract(c, carry):
            rows = rows_of(c, size)

            def probs_of(h, q, keys):
                return p_ref[c, h]

            back_tract(c, rows, heads, ids_ref, enc_ref, None, v_ref, q_ref, ga_ref,
                       probs_of, acc_k, acc_v, None)
            return carry

        lax.fori_loop(0, tracts, tract, 0)
        sk_ref[...] = jnp.transpose(acc_k[...]).astype(BF)
        sv_ref[...] = jnp.transpose(acc_v[...]).astype(BF)

    @pl.when(s != 0)
    def _():
        sk_ref[...] = lk_ref[...]
        sv_ref[...] = lv_ref[...]


def relay_kernel(from_section, combine, *refs):
    part_ref, row_refs, full_ref = refs[0], refs[1:-8], refs[-8]
    rs, done, rs_s, rs_r, ag_s, ag_r = refs[-7:-1]
    s = lax.axis_index("section")
    m = lax.axis_index("mp")
    count = len(OFFSETS)
    there = {"section": 1 - s}
    everyone = [{"mp": to_peer(m, k)} for k in range(count)]
    everyone += [{"mp": to_peer(m, k), "section": 1 - s} for k in range(count)]
    greet(everyone + [there])
    shard = rs.shape[1]
    mine = rows_of(m, shard)

    @pl.when(s == from_section)
    def _():
        sends = []
        for k in range(count):
            p = to_peer(m, k)
            sends.append(remote(part_ref.at[rows_of(p, shard), :], rs.at[k],
                                rs_s.at[k], rs_r.at[k], {"mp": p}))
            sends[-1].start()
        total = part_ref[mine, :].astype(F32)
        for k in range(count):
            p = from_peer(m, k)
            remote(part_ref.at[rows_of(p, shard), :], rs.at[k],
                   rs_s.at[k], rs_r.at[k], {"mp": p}).wait_recv()
            total = total + rs[k].astype(F32)
        done[...] = combine(total, mine, *row_refs).astype(BF)
        for k in range(count + 1):
            device = there if k == count else {"mp": to_peer(m, k), "section": 1 - s}
            sends.append(remote(done, full_ref.at[mine, :], ag_s.at[k], ag_r.at[k], device))
            sends[-1].start()
        for copy in sends:
            copy.wait_send()

    @pl.when(s != from_section)
    def _():
        for k in range(count + 1):
            p = m if k == count else from_peer(m, k)
            device = there if k == count else {"mp": p, "section": 1 - s}
            remote(done, full_ref.at[rows_of(p, shard), :],
                   ag_s.at[k], ag_r.at[k], device).wait_recv()


def relay(from_section, combine, part, rows, ident, peers):
    dma = pltpu.SemaphoreType.DMA
    count = len(OFFSETS)
    vmem = pl.BlockSpec(memory_space=VMEM)
    shard = part.shape[0] // peers
    return pl.pallas_call(
        functools.partial(relay_kernel, from_section, combine),
        name="relay_%d" % ident,
        out_shape=jax.ShapeDtypeStruct(part.shape, BF),
        in_specs=[vmem] * (1 + len(rows)),
        out_specs=vmem,
        scratch_shapes=[
            VMEM((count, shard, part.shape[1]), BF), VMEM((shard, part.shape[1]), BF),
            dma((count,)), dma((count,)), dma((count + 1,)), dma((count + 1,)),
            VMEM((8, 128), F32),
        ],
        compiler_params=pltpu.CompilerParams(
            collective_id=ident, has_side_effects=True, vmem_limit_bytes=LIMIT),
    )(part, *rows)


def forward_rows(total, mine, x_ref):
    return x_ref[mine, :].astype(F32) + total


def backward_rows(total, mine, a_ref, g_ref, gain_ref):
    wide = a_ref[mine, :].astype(F32)
    inv = rms_scale(wide)
    gain = gain_ref[...]
    normed = (wide * inv * gain).astype(BF).astype(F32)
    row_total = jnp.sum(normed * total, axis=-1, keepdims=True)
    return (g_ref[mine, :].astype(F32) + inv * gain * total
            - wide * (inv * inv * row_total / wide.shape[1]))


def settle_kernel(k_ref, v_ref, ok_ref, ov_ref, rs, rs_s, rs_r, ag_s, ag_r):
    d = lax.axis_index("dp")
    count = SIDE - 1
    steps = (2, 1, 3)
    greet([{"dp": lax.rem(d + step, SIDE)} for step in steps])
    quarter = rs.shape[2]
    sends = []
    for k in range(count):
        p = lax.rem(d + steps[k], SIDE)
        for i, ref in enumerate((k_ref, v_ref)):
            sends.append(remote(ref.at[rows_of(p, quarter), :], rs.at[k, i],
                                rs_s.at[k, i], rs_r.at[k, i], {"dp": p}))
            sends[-1].start()
    mine = rows_of(d, quarter)
    for i, (ref, out) in enumerate(((k_ref, ok_ref), (v_ref, ov_ref))):
        total = ref[mine, :].astype(F32)
        for k in range(count):
            p = lax.rem(d + SIDE - steps[k], SIDE)
            remote(ref.at[mine, :], rs.at[k, i], rs_s.at[k, i], rs_r.at[k, i], {"dp": p}).wait_recv()
            total = total + rs[k, i].astype(F32)
        out[mine, :] = total.astype(BF)
        for k in range(count):
            p = lax.rem(d + steps[k], SIDE)
            sends.append(remote(out.at[mine, :], out.at[mine, :],
                                ag_s.at[k, i], ag_r.at[k, i], {"dp": p}))
            sends[-1].start()
    for i, out in enumerate((ok_ref, ov_ref)):
        for k in range(count):
            p = lax.rem(d + SIDE - steps[k], SIDE)
            there = rows_of(p, quarter)
            remote(out.at[there, :], out.at[there, :], ag_s.at[k, i], ag_r.at[k, i], {"dp": p}).wait_recv()
    for copy in sends:
        copy.wait_send()


def settle(keys, values):
    dma = pltpu.SemaphoreType.DMA
    vmem = pl.BlockSpec(memory_space=VMEM)
    count = SIDE - 1
    return pl.pallas_call(
        settle_kernel,
        name="settle",
        out_shape=(jax.ShapeDtypeStruct(keys.shape, BF),) * 2,
        in_specs=[vmem] * 2,
        out_specs=(vmem,) * 2,
        scratch_shapes=[VMEM((count, 2, keys.shape[0] // SIDE, keys.shape[1]), BF)]
        + [dma((count, 2))] * 4,
        compiler_params=pltpu.CompilerParams(
            collective_id=3, has_side_effects=True, vmem_limit_bytes=LIMIT),
    )(keys, values)


def local(kernel, name, outs, args, scalars, scratch=()):
    vmem = pl.BlockSpec(memory_space=VMEM)
    smem = pl.BlockSpec(memory_space=pltpu.SMEM)
    return pl.pallas_call(
        kernel,
        name=name,
        out_shape=tuple(jax.ShapeDtypeStruct(*o) for o in outs),
        in_specs=[smem] * scalars + [vmem] * (len(args) - scalars),
        out_specs=(vmem,) * len(outs),
        scratch_shapes=list(scratch),
        compiler_params=pltpu.CompilerParams(vmem_limit_bytes=LIMIT),
    )(*args)


def on_device(
    segment_input,
    out_grad,
    pool_tokens,
    neighbour_ids,
    neighbour_counts,
    enc_gain,
    enc_up,
    enc_down,
    norm_gain,
    w_query,
    w_key,
    w_value,
    w_out,
):
    peers = lax.axis_size("mp")
    s = lax.axis_index("section")
    micro, _, row_count, feat = segment_input.shape
    rows = micro * row_count
    width = feat * peers
    enc = pool_tokens.shape[3]
    head_width = w_query.shape[2]
    heads = head_width // HEAD
    tracts = micro * neighbour_ids.shape[2]
    slots = neighbour_ids.shape[3]
    size = rows // tracts
    ids = neighbour_ids[:, 0].reshape(tracts, slots)
    used = neighbour_counts[:, 0].reshape(tracts)
    x_own = jnp.where(s == 0, segment_input[:, 0], out_grad[:, 0]).reshape(rows, feat)
    pool = pool_tokens[:, 0].reshape(-1, enc)
    down = jnp.transpose(enc_down.reshape(peers, head_width, -1), (0, 2, 1))
    down = jnp.pad(down, ((0, 0), (0, -down.shape[1] % 16), (0, 0)))
    wq, wk, wv = w_query[0], w_key[0], w_value[0]

    encoded, x_full, wo_rows = encode(x_own, w_out[0], down, pool, enc_gain[None], enc_up)
    shape_q = ((rows, head_width), BF)
    shape_kv = ((encoded.shape[0], head_width), BF)
    keys, values, queries, probs, part, grad_att = local(
        front_kernel, "front",
        [shape_kv, shape_kv, shape_q, ((tracts, heads, size, slots * NT), F32),
         ((rows, width), BF), shape_q],
        (ids, used, x_full, norm_gain, wq, encoded, wk, wv, wo_rows), 2)
    acts = relay(0, forward_rows, part, (x_full,), 1, peers)
    shape_w = ((enc, head_width), BF)
    accs = [VMEM((head_width, enc), F32)] * 2
    part_back, late_k, late_v = local(
        late_kernel, "late",
        [((rows, width), BF), shape_w, shape_w],
        (ids, used, acts, norm_gain, wq, encoded, keys, values, grad_att), 2,
        [VMEM(*shape_q)] + accs)
    grads = relay(1, backward_rows, part_back, (acts, x_full, norm_gain), 2, peers)
    sum_k, sum_v = local(
        early_kernel, "early",
        [shape_w, shape_w],
        (ids, grads, wo_rows, encoded, values, queries, probs, late_k, late_v), 1,
        [VMEM(*shape_q)] + accs)
    grad_k, grad_v = settle(sum_k, sum_v)
    return (grad_k[None], grad_v[None])


def solution(mesh):
    placed = (
        P(None, "dp", None, "mp"),
        P(None, "dp", None, "mp"),
        P("section", "dp", None, None),
        P(None, "dp", None, None),
        P(None, "dp", None),
        P(),
        P(None, "mp"),
        P(None, "mp"),
        P("section", None),
        P("section", None, "mp"),
        P("section", None, "mp"),
        P("section", None, "mp"),
        P("section", None, "mp"),
    )
    return jax.shard_map(
        on_device,
        mesh=mesh,
        in_specs=placed,
        out_specs=(P("section", None, "mp"), P("section", None, "mp")),
        check_vma=False,
    )
```

```python
import functools

import jax
import jax.numpy as jnp
from jax import lax
from jax.experimental import pallas as pl
from jax.experimental.pallas import tpu as pltpu
from jax.sharding import PartitionSpec as P

HEAD = 128
NT = 128
SIDE = 4
EPSILON = 1e-05
SCALE = HEAD ** (-0.5)
VMEM = pltpu.VMEM
BF = jnp.bfloat16
F32 = jnp.float32
LIMIT = 60 * 1024 * 1024

OFFSETS = [(2, 2), (2, 1), (2, 3), (1, 2), (3, 2), (1, 1), (3, 3), (1, 3), (3, 1),
           (2, 0), (0, 2), (1, 0), (0, 1), (3, 0), (0, 3)]


def dims(lhs, rhs):
    return (((lhs,), (rhs,)), ((), ()))


def mul(a, b, lhs=1, rhs=0):
    return lax.dot_general(a, b, dims(lhs, rhs), preferred_element_type=F32)


def rms_scale(values):
    return lax.rsqrt(jnp.mean(values * values, axis=-1, keepdims=True) + EPSILON)


def shifted(m, dz, dy):
    z = lax.rem(lax.div(m, SIDE) + dz, SIDE)
    y = lax.rem(lax.rem(m, SIDE) + dy, SIDE)
    return z * SIDE + y


def to_peer(m, k):
    return shifted(m, *OFFSETS[k])


def from_peer(m, k):
    dz, dy = OFFSETS[k]
    return shifted(m, (SIDE - dz) % SIDE, (SIDE - dy) % SIDE)


def remote(src, dst, send, recv, device):
    return pltpu.make_async_remote_copy(
        src_ref=src, dst_ref=dst, send_sem=send, recv_sem=recv,
        device_id=device, device_id_type=pl.DeviceIdType.MESH,
    )


def greet(devices):
    barrier = pltpu.get_barrier_semaphore()
    for device in devices:
        pl.semaphore_signal(
            barrier, inc=1, device_id=device, device_id_type=pl.DeviceIdType.MESH
        )
    pl.semaphore_wait(barrier, len(devices))


def rows_of(index, size):
    return pl.ds(pl.multiple_of(index * size, size), size)


def near(m, axis, step):
    return shifted(m, step % SIDE, 0) if axis == "z" else shifted(m, 0, step % SIDE)


def place(m, h, first, second):
    if h == 0:
        return shifted(m, second % SIDE, first % SIDE)
    return shifted(m, first % SIDE, second % SIDE)


AXES = (("y", "z"), ("z", "y"))
ARRIVALS = [(-1, 0), (1, 0), (0, -1), (0, 1), (2, 0), (-1, -1), (-1, 1), (1, -1), (1, 1),
            (0, 2), (2, -1), (2, 1), (-1, 2), (1, 2), (2, 2)]


class Spread:
    def __init__(self, m, slot, recv, send, landed=None):
        self.m, self.slot, self.recv, self.send = m, slot, recv, send
        self.landed = landed
        self.sends = []
        self.step = 0

    def put(self, h, a, b, q, which, by, device=None, source=None):
        origin = place(self.m, h, a, b)
        there = (a - by, b) if which == 0 else (a, b - by)
        key = (there[0] % SIDE) * SIDE + there[1] % SIDE
        ref = self.slot(origin, h, q)
        target = {"mp": near(self.m, AXES[h][which], by)}
        if device:
            target.update(device)
        copy = remote(ref if source is None else source(h), ref, self.send.at[len(self.sends)],
                      self.recv.at[h, key, q or 0], target)
        copy.start()
        self.sends.append(copy)

    def own(self, device=None, source=None):
        for which in (0, 1):
            for h in (0, 1):
                for by in (1, -1):
                    self.put(h, 0, 0, None, which, by, device, source)

    def take(self, h, a, b, q):
        ref = self.slot(place(self.m, h, a, b), h, q)
        key = (a % SIDE) * SIDE + b % SIDE
        remote(ref, ref, self.send.at[0], self.recv.at[h, key, q or 0],
               {"mp": near(self.m, "y", 1)}).wait_recv()

    def pass_on(self, until=len(ARRIVALS)):
        for a, b in ARRIVALS[self.step:until]:
            for h in (0, 1):
                if b == 2 or (b == 0 and a == 2):
                    self.take(h, a, b, 0)
                    self.take(h, a, b, 1)
                else:
                    self.take(h, a, b, None)
                if b == 0:
                    if a == -1:
                        self.put(h, a, b, 0, 0, 1)
                    if a == 1:
                        self.put(h, a, b, 1, 0, -1)
                    self.put(h, a, b, None, 1, 1)
                    self.put(h, a, b, None, 1, -1)
                if b == -1:
                    self.put(h, a, b, 0, 1, 1)
                if b == 1:
                    self.put(h, a, b, 1, 1, -1)
                if self.landed:
                    self.landed(h, a, b)
        self.step = until

    def close(self):
        for copy in self.sends:
            copy.wait_send()


ORDER = (2, 1, 3, 0)
DIRS = (1, -1)


def gather_sum_scratch(quarter):
    dma = pltpu.SemaphoreType.DMA
    return [
        VMEM((2, 2, SIDE) + quarter, BF), VMEM((2, 2, 2, SIDE) + quarter, BF),
        VMEM((2, 2, SIDE) + quarter, BF),
        VMEM((2, 2) + quarter, BF), VMEM((2, 2, 2) + quarter, BF), VMEM((2, 2) + quarter, BF),
        VMEM((2, 2, SIDE) + quarter, BF),
        dma((2, 2, SIDE)), dma((2, 2, 2, SIDE)), dma((2, 2)), dma((2, 2, 2)), dma((64,)),
    ]


def gather_sum(m, slot, load, scratch, begin=None):
    far1, near1, add1, far2, near2, add2, mid, far1_r, near1_r, far2_r, near2_r, send = scratch
    sends = []

    def put(src, dst, recv, h, which, by):
        copy = remote(src, dst, send.at[len(sends)], recv, {"mp": near(m, AXES[h][which], by)})
        copy.start()
        sends.append(copy)

    def take(dst, recv):
        remote(dst, dst, send.at[0], recv, {"mp": near(m, "y", 1)}).wait_recv()

    def owner(h, a, b):
        return place(m, h, a, b)

    for b in ORDER:
        if begin:
            begin(b)
        for h in (0, 1):
            for i, by in enumerate(DIRS):
                put(slot(owner(h, 2, b), h, i), far1.at[h, i, b], far1_r.at[h, i, b], h, 0, by)
        for h in (0, 1):
            for i, by in enumerate(DIRS):
                put(slot(owner(h, by, b), h, 1 - i), near1.at[h, i, 1 - i, b],
                    near1_r.at[h, i, 1 - i, b], h, 0, by)
    for b in ORDER:
        for h in (0, 1):
            for i, by in enumerate(DIRS):
                take(far1.at[h, i, b], far1_r.at[h, i, b])
                add1[h, i, b] = (far1[h, i, b].astype(F32)
                                 + load(owner(h, by, b), h, i).astype(F32)).astype(BF)
                put(add1.at[h, i, b], near1.at[h, i, i, b], near1_r.at[h, i, i, b], h, 0, by)

    def first(h, q, b):
        total = load(owner(h, 0, b), h, q).astype(F32)
        for i in (0, 1):
            take(near1.at[h, i, q, b], near1_r.at[h, i, q, b])
            total = total + near1[h, i, q, b].astype(F32)
        return total

    for b in ORDER[:3]:
        for h in (0, 1):
            for q in (1, 0):
                mid[h, q, b] = first(h, q, b).astype(BF)
                if b == 2:
                    put(mid.at[h, q, b], far2.at[h, q], far2_r.at[h, q], h, 1, DIRS[q])
                else:
                    i = 0 if b == 1 else 1
                    if q != i:
                        put(mid.at[h, q, b], near2.at[h, i, q], near2_r.at[h, i, q], h, 1, DIRS[i])
    for h in (0, 1):
        for i, by in enumerate(DIRS):
            take(far2.at[h, i], far2_r.at[h, i])
            add2[h, i] = (far2[h, i].astype(F32) + mid[h, i, by % SIDE].astype(F32)).astype(BF)
            put(add2.at[h, i], near2.at[h, i, i], near2_r.at[h, i, i], h, 1, by)
    sums = {}
    for h in (0, 1):
        for q in (0, 1):
            sums[h, q] = first(h, q, 0)
    for h in (0, 1):
        for q in (0, 1):
            for i in (0, 1):
                take(near2.at[h, i, q], near2_r.at[h, i, q])
                sums[h, q] = sums[h, q] + near2[h, i, q].astype(F32)
    return sums, sends


def neighbours_of(m):
    return [near(m, axis, by) for axis in ("y", "z") for by in (1, -1)]


def encode_kernel(
    x_ref, wo_ref, ed_ref, pool_ref, gain_ref, up_ref,
    enc_ref, xf_ref, wor_ref,
    edr, dt, hid, part,
    own_sem, ed_s, ed_r, wo_s, wo_r, x_s, x_r, ag_s, ag_r, fw_s, fw_r, *scratch,
):
    s = lax.axis_index("section")
    m = lax.axis_index("mp")
    other = {"section": 1 - s}
    count = len(OFFSETS)
    greet([{"mp": to_peer(m, k)} for k in range(count)] + [other])
    span = wor_ref.shape[0]
    cols = rows_of(m, HEAD)
    own = [
        pltpu.make_async_copy(x_ref, xf_ref.at[:, cols], own_sem.at[0]),
        pltpu.make_async_copy(wo_ref.at[rows_of(m, span), :], wor_ref.at[:, cols], own_sem.at[1]),
        pltpu.make_async_copy(ed_ref.at[m], edr.at[m], own_sem.at[2]),
    ]
    for copy in own:
        copy.start()
    sends = []
    for k in range(count):
        p = to_peer(m, k)
        sends.append(remote(ed_ref.at[p], edr.at[m], ed_s.at[k], ed_r.at[k], {"mp": p}))
        sends[-1].start()
    for k in range(count):
        p = to_peer(m, k)
        sends.append(remote(wo_ref.at[rows_of(p, span), :], wor_ref.at[:, cols],
                            wo_s.at[k], wo_r.at[k], {"mp": p}))
        sends[-1].start()

    tall = x_ref.shape[0]

    def x_rows(h, q):
        if q is None:
            return pl.ds(h * (tall // 2), tall // 2)
        return pl.ds((2 * h + q) * (tall // 4), tall // 4)

    xs = Spread(m, lambda owner, h, q: xf_ref.at[x_rows(h, q), rows_of(owner, HEAD)], x_r, x_s)
    xs.own(None, lambda h: x_ref.at[x_rows(h, None), :])
    gain = gain_ref[...]

    def hidden_rows(i, carry):
        rows = rows_of(i, 256)
        wide = pool_ref[rows, :].astype(F32)
        normed = (wide * rms_scale(wide) * gain).astype(BF)
        hid[rows, :] = jax.nn.gelu(mul(normed, up_ref[...])).astype(BF)
        return carry

    lax.fori_loop(0, SIDE, hidden_rows, 0)

    own[2].wait()
    for k in range(count):
        p = from_peer(m, k)
        remote(ed_ref.at[p], edr.at[p], ed_s.at[k], ed_r.at[k], {"mp": p}).wait_recv()
    feat = enc_ref.shape[1] // len(edr)
    for p in range(len(edr)):
        dt[pl.ds(p * feat, feat), :] = edr[p, pl.ds(0, feat), :].astype(F32)
    down = dt[...].astype(BF)
    shard = part.shape[0] // len(edr)

    def rows_at(owner, h, q, base=0):
        if q is None:
            return pl.ds(pl.multiple_of((base + owner) * shard + h * (shard // 2), shard // 2),
                         shard // 2)
        return pl.ds(pl.multiple_of((base + owner) * shard + (2 * h + q) * (shard // 4), shard // 4),
                     shard // 4)

    def some(i, carry):
        block = rows_of(i, SIDE * shard)
        part[block, :] = mul(hid[block, :], down, 1, 1).astype(BF)
        return carry

    lax.fori_loop(0, SIDE, some, 0)
    xs.pass_on(5)
    sums, more = gather_sum(m, lambda owner, h, q: part.at[rows_at(owner, h, q), :],
                            lambda owner, h, q: part[rows_at(owner, h, q), :], scratch)
    half = s * len(edr)

    def enc_slot(owner, h, q):
        return enc_ref.at[rows_at(owner, h, q, half), :]

    for h in (0, 1):
        for q in (0, 1):
            total = pool_ref[rows_at(m, h, q), :].astype(F32) + sums[h, q]
            enc_ref[rows_at(m, h, q, half), :] = total.astype(BF)

    def to_other(h, a, b):
        key = (a % SIDE) * SIDE + b % SIDE
        ref = enc_slot(place(m, h, a, b), h, None)
        more.append(remote(ref, ref, fw_s.at[h, key], fw_r.at[h, key], other))
        more[-1].start()

    spread = Spread(m, enc_slot, ag_r, ag_s, to_other)
    spread.own()
    to_other(0, 0, 0)
    to_other(1, 0, 0)
    spread.pass_on(5)
    xs.pass_on(9)
    spread.pass_on(9)
    xs.pass_on()
    spread.pass_on()
    away = (1 - s) * len(edr)
    for a, b in [(0, 0)] + ARRIVALS:
        for h in (0, 1):
            key = (a % SIDE) * SIDE + b % SIDE
            ref = enc_ref.at[rows_at(place(m, h, a, b), h, None, away), :]
            remote(ref, ref, fw_s.at[h, key], fw_r.at[h, key], other).wait_recv()
    for k in range(count):
        p = from_peer(m, k)
        there = rows_of(p, HEAD)
        remote(wo_ref.at[rows_of(p, span), :], wor_ref.at[:, there],
               wo_s.at[k], wo_r.at[k], {"mp": p}).wait_recv()
    own[0].wait()
    own[1].wait()
    for copy in sends + more:
        copy.wait_send()
    spread.close()
    xs.close()


def encode(x, wo, ed, pool, gain, up):
    peers, _, span = ed.shape
    rows, enc = pool.shape
    dma = pltpu.SemaphoreType.DMA
    count = len(OFFSETS)
    vmem = pl.BlockSpec(memory_space=VMEM)
    hbm = pl.BlockSpec(memory_space=pl.ANY)
    return pl.pallas_call(
        encode_kernel,
        name="encode_exchange",
        out_shape=(
            jax.ShapeDtypeStruct((2 * rows, enc), BF),
            jax.ShapeDtypeStruct((x.shape[0], x.shape[1] * peers), BF),
            jax.ShapeDtypeStruct((span, wo.shape[1] * peers), BF),
        ),
        in_specs=[hbm, hbm, hbm, vmem, vmem, vmem],
        out_specs=(vmem,) * 3,
        scratch_shapes=[
            VMEM(ed.shape, BF), VMEM((enc, span), F32), VMEM((rows, span), BF),
            VMEM((rows, enc), BF),
            dma((3,)),
        ] + [dma((count,))] * 4 + [dma((40,)), dma((2, 16, 2))] * 2 + [dma((2, 16))] * 2
        + gather_sum_scratch((rows // peers // 4, enc)),
        compiler_params=pltpu.CompilerParams(
            collective_id=0, has_side_effects=True, vmem_limit_bytes=LIMIT),
    )(x, wo, ed, pool, gain, up)


def head_cols(h):
    return pl.ds(h * HEAD, HEAD)


def gathered(ref, ids_ref, c, columns):
    slots = ids_ref.shape[1]
    return jnp.concatenate(
        [ref[rows_of(ids_ref[c, j], NT), columns] for j in range(slots)], axis=0)


def soft(scores, used):
    slot = lax.div(lax.broadcasted_iota(jnp.int32, scores.shape, 1), NT)
    scores = jnp.where(slot < used, scores, -1e30)
    grown = jnp.exp(scores - jnp.max(scores, axis=-1, keepdims=True))
    return grown / jnp.sum(grown, axis=-1, keepdims=True)


def queries_of(x_ref, gain_ref, wq_ref, q_ref):
    def some(i, carry):
        rows = rows_of(i, 256)
        wide = x_ref[rows, :].astype(F32)
        normed = (wide * rms_scale(wide) * gain_ref[...]).astype(BF)
        q_ref[rows, :] = (mul(normed, wq_ref[...]) * SCALE).astype(BF)
        return carry

    lax.fori_loop(0, x_ref.shape[0] // 256, some, 0)


def grad_attended(x_ref, wor_ref, ga_ref):
    def some(i, carry):
        rows = rows_of(i, 256)
        ga_ref[rows, :] = mul(x_ref[rows, :], wor_ref[...], 1, 1).astype(BF)
        return carry

    lax.fori_loop(0, x_ref.shape[0] // 256, some, 0)


def front_kernel(ids_ref, used_ref, x_ref, gain_ref, wq_ref, enc_ref, wk_ref, wv_ref, wor_ref,
                 k_ref, v_ref, q_ref, p_ref, part_ref, ga_ref):
    s = lax.axis_index("section")

    def project(i, carry):
        rows = rows_of(i, 512)
        block = enc_ref[rows, :]
        k_ref[rows, :] = mul(block, wk_ref[...]).astype(BF)
        v_ref[rows, :] = mul(block, wv_ref[...]).astype(BF)
        return carry

    lax.fori_loop(0, enc_ref.shape[0] // 512, project, 0)
    heads = q_ref.shape[1] // HEAD
    tracts = ids_ref.shape[0]
    size = x_ref.shape[0] // tracts

    @pl.when(s == 0)
    def _():
        queries_of(x_ref, gain_ref, wq_ref, q_ref)

        def tract(c, carry):
            rows = rows_of(c, size)
            found = []
            for h in range(heads):
                keys = gathered(k_ref, ids_ref, c, head_cols(h))
                probs = soft(mul(q_ref[rows, head_cols(h)], keys, 1, 1), used_ref[c])
                p_ref[c, h] = probs
                values = gathered(v_ref, ids_ref, c, head_cols(h))
                found.append(mul(probs.astype(BF), values).astype(BF))
            part_ref[rows, :] = mul(jnp.concatenate(found, axis=1), wor_ref[...]).astype(BF)
            return carry

        lax.fori_loop(0, tracts, tract, 0)

    @pl.when(s != 0)
    def _():
        grad_attended(x_ref, wor_ref, ga_ref)


def back_tract(c, rows, heads, ids_ref, enc_ref, k_ref, v_ref, q_ref, ga_ref, probs_of, acc_k, acc_v,
               scores_used):
    near = gathered(enc_ref, ids_ref, c, slice(None))
    key_t, value_t, query_g = [], [], []
    for h in range(heads):
        q = q_ref[rows, head_cols(h)]
        ga = ga_ref[rows, head_cols(h)]
        values = gathered(v_ref, ids_ref, c, head_cols(h))
        keys = None
        if k_ref is not None:
            keys = gathered(k_ref, ids_ref, c, head_cols(h))
        probs = probs_of(h, q, keys)
        grad_probs = mul(ga, values, 1, 1)
        grad_scores = probs * (grad_probs - jnp.sum(probs * grad_probs, axis=-1, keepdims=True))
        grad_scores = grad_scores.astype(BF)
        value_t.append(mul(ga, probs.astype(BF), 0, 0).astype(BF))
        key_t.append(mul(q, grad_scores, 0, 0).astype(BF))
        if keys is not None:
            query_g.append((mul(grad_scores, keys) * SCALE).astype(BF))
    acc_k[...] += mul(jnp.concatenate(key_t, axis=0), near)
    acc_v[...] += mul(jnp.concatenate(value_t, axis=0), near)
    return query_g


def late_kernel(ids_ref, used_ref, x_ref, gain_ref, wq_ref, enc_ref, k_ref, v_ref, ga_ref,
                part_ref, sk_ref, sv_ref, q_ref, acc_k, acc_v):
    heads = q_ref.shape[1] // HEAD
    tracts = ids_ref.shape[0]
    size = x_ref.shape[0] // tracts

    @pl.when(lax.axis_index("section") != 0)
    def _():
        queries_of(x_ref, gain_ref, wq_ref, q_ref)
        acc_k[...] = jnp.zeros_like(acc_k)
        acc_v[...] = jnp.zeros_like(acc_v)

        def tract(c, carry):
            rows = rows_of(c, size)

            def probs_of(h, q, keys):
                return soft(mul(q, keys, 1, 1), used_ref[c])

            query_g = back_tract(c, rows, heads, ids_ref, enc_ref, k_ref, v_ref, q_ref, ga_ref,
                                 probs_of, acc_k, acc_v, None)
            part_ref[rows, :] = mul(jnp.concatenate(query_g, axis=1), wq_ref[...], 1, 1).astype(BF)
            return carry

        lax.fori_loop(0, tracts, tract, 0)
        sk_ref[...] = jnp.transpose(acc_k[...]).astype(BF)
        sv_ref[...] = jnp.transpose(acc_v[...]).astype(BF)


def early_kernel(ids_ref, g_ref, wor_ref, enc_ref, v_ref, q_ref, p_ref, lk_ref, lv_ref,
                 sk_ref, sv_ref, ga_ref, acc_k, acc_v):
    heads = q_ref.shape[1] // HEAD
    tracts = ids_ref.shape[0]
    size = g_ref.shape[0] // tracts
    s = lax.axis_index("section")

    @pl.when(s == 0)
    def _():
        grad_attended(g_ref, wor_ref, ga_ref)
        acc_k[...] = jnp.zeros_like(acc_k)
        acc_v[...] = jnp.zeros_like(acc_v)

        def tract(c, carry):
            rows = rows_of(c, size)

            def probs_of(h, q, keys):
                return p_ref[c, h]

            back_tract(c, rows, heads, ids_ref, enc_ref, None, v_ref, q_ref, ga_ref,
                       probs_of, acc_k, acc_v, None)
            return carry

        lax.fori_loop(0, tracts, tract, 0)
        sk_ref[...] = jnp.transpose(acc_k[...]).astype(BF)
        sv_ref[...] = jnp.transpose(acc_v[...]).astype(BF)

    @pl.when(s != 0)
    def _():
        sk_ref[...] = lk_ref[...]
        sv_ref[...] = lv_ref[...]


def relay_kernel(from_section, combine, *refs):
    outer = len(refs) - 1 - 12 - 5
    part_ref, row_refs, full_ref = refs[0], refs[1:outer], refs[outer]
    done, hand_s, hand_r, ag_s, ag_r = refs[outer + 1:outer + 6]
    scratch = refs[outer + 6:]
    s = lax.axis_index("section")
    m = lax.axis_index("mp")
    there = {"section": 1 - s}
    greet([{"mp": p} for p in neighbours_of(m)]
          + [{"mp": p, "section": 1 - s} for p in neighbours_of(m)] + [there])
    shard, width = done.shape
    mine = rows_of(m, shard)

    def columns(h, q):
        if q is None:
            return pl.ds(h * (width // 2), width // 2)
        return pl.ds((2 * h + q) * (width // 4), width // 4)

    def slot(ref):
        return lambda owner, h, q: ref.at[rows_of(owner, shard), columns(h, q)]

    @pl.when(s == from_section)
    def _():
        sums, sends = gather_sum(m, slot(part_ref),
                                 lambda owner, h, q: part_ref[rows_of(owner, shard), columns(h, q)],
                                 scratch)
        total = jnp.concatenate([sums[h, q] for h in (0, 1) for q in (0, 1)], axis=1)
        done[...] = combine(total, mine, *row_refs).astype(BF)
        spread = Spread(m, slot(full_ref), ag_r, ag_s)
        spread.own(there, lambda h: done.at[:, columns(h, None)])
        hand = remote(done, full_ref.at[mine, :], hand_s.at[0], hand_r.at[0], there)
        hand.start()
        for copy in sends + [hand]:
            copy.wait_send()
        spread.close()

    @pl.when(s != from_section)
    def _():
        spread = Spread(m, slot(full_ref), ag_r, ag_s)
        spread.pass_on()
        remote(done, full_ref.at[mine, :], hand_s.at[0], hand_r.at[0], there).wait_recv()
        spread.close()


def relay(from_section, combine, part, rows, ident, peers):
    dma = pltpu.SemaphoreType.DMA
    vmem = pl.BlockSpec(memory_space=VMEM)
    shard, width = part.shape[0] // peers, part.shape[1]
    return pl.pallas_call(
        functools.partial(relay_kernel, from_section, combine),
        name="relay_%d" % ident,
        out_shape=jax.ShapeDtypeStruct(part.shape, BF),
        in_specs=[vmem] * (1 + len(rows)),
        out_specs=vmem,
        scratch_shapes=[VMEM((shard, width), BF), dma((1,)), dma((1,)), dma((40,)),
                        dma((2, 16, 2))] + gather_sum_scratch((shard, width // 4)),
        compiler_params=pltpu.CompilerParams(
            collective_id=ident, has_side_effects=True, vmem_limit_bytes=LIMIT),
    )(part, *rows)


def forward_rows(total, mine, x_ref):
    return x_ref[mine, :].astype(F32) + total


def backward_rows(total, mine, a_ref, g_ref, gain_ref):
    wide = a_ref[mine, :].astype(F32)
    inv = rms_scale(wide)
    gain = gain_ref[...]
    normed = (wide * inv * gain).astype(BF).astype(F32)
    row_total = jnp.sum(normed * total, axis=-1, keepdims=True)
    return (g_ref[mine, :].astype(F32) + inv * gain * total
            - wide * (inv * inv * row_total / wide.shape[1]))


def settle_kernel(k_ref, v_ref, ok_ref, ov_ref, rs, rs_s, rs_r, ag_s, ag_r):
    d = lax.axis_index("dp")
    count = SIDE - 1
    steps = (2, 1, 3)
    greet([{"dp": lax.rem(d + step, SIDE)} for step in steps])
    quarter = rs.shape[2]
    sends = []
    for k in range(count):
        p = lax.rem(d + steps[k], SIDE)
        for i, ref in enumerate((k_ref, v_ref)):
            sends.append(remote(ref.at[rows_of(p, quarter), :], rs.at[k, i],
                                rs_s.at[k, i], rs_r.at[k, i], {"dp": p}))
            sends[-1].start()
    mine = rows_of(d, quarter)
    for i, (ref, out) in enumerate(((k_ref, ok_ref), (v_ref, ov_ref))):
        total = ref[mine, :].astype(F32)
        for k in range(count):
            p = lax.rem(d + SIDE - steps[k], SIDE)
            remote(ref.at[mine, :], rs.at[k, i], rs_s.at[k, i], rs_r.at[k, i], {"dp": p}).wait_recv()
            total = total + rs[k, i].astype(F32)
        out[mine, :] = total.astype(BF)
        for k in range(count):
            p = lax.rem(d + steps[k], SIDE)
            sends.append(remote(out.at[mine, :], out.at[mine, :],
                                ag_s.at[k, i], ag_r.at[k, i], {"dp": p}))
            sends[-1].start()
    for i, out in enumerate((ok_ref, ov_ref)):
        for k in range(count):
            p = lax.rem(d + SIDE - steps[k], SIDE)
            there = rows_of(p, quarter)
            remote(out.at[there, :], out.at[there, :], ag_s.at[k, i], ag_r.at[k, i], {"dp": p}).wait_recv()
    for copy in sends:
        copy.wait_send()


def settle(keys, values):
    dma = pltpu.SemaphoreType.DMA
    vmem = pl.BlockSpec(memory_space=VMEM)
    count = SIDE - 1
    return pl.pallas_call(
        settle_kernel,
        name="settle",
        out_shape=(jax.ShapeDtypeStruct(keys.shape, BF),) * 2,
        in_specs=[vmem] * 2,
        out_specs=(vmem,) * 2,
        scratch_shapes=[VMEM((count, 2, keys.shape[0] // SIDE, keys.shape[1]), BF)]
        + [dma((count, 2))] * 4,
        compiler_params=pltpu.CompilerParams(
            collective_id=3, has_side_effects=True, vmem_limit_bytes=LIMIT),
    )(keys, values)


def local(kernel, name, outs, args, scalars, scratch=()):
    vmem = pl.BlockSpec(memory_space=VMEM)
    smem = pl.BlockSpec(memory_space=pltpu.SMEM)
    return pl.pallas_call(
        kernel,
        name=name,
        out_shape=tuple(jax.ShapeDtypeStruct(*o) for o in outs),
        in_specs=[smem] * scalars + [vmem] * (len(args) - scalars),
        out_specs=(vmem,) * len(outs),
        scratch_shapes=list(scratch),
        compiler_params=pltpu.CompilerParams(vmem_limit_bytes=LIMIT),
    )(*args)


def on_device(
    segment_input,
    out_grad,
    pool_tokens,
    neighbour_ids,
    neighbour_counts,
    enc_gain,
    enc_up,
    enc_down,
    norm_gain,
    w_query,
    w_key,
    w_value,
    w_out,
):
    peers = lax.axis_size("mp")
    s = lax.axis_index("section")
    micro, _, row_count, feat = segment_input.shape
    rows = micro * row_count
    width = feat * peers
    enc = pool_tokens.shape[3]
    head_width = w_query.shape[2]
    heads = head_width // HEAD
    tracts = micro * neighbour_ids.shape[2]
    slots = neighbour_ids.shape[3]
    size = rows // tracts
    ids = neighbour_ids[:, 0].reshape(tracts, slots)
    used = neighbour_counts[:, 0].reshape(tracts)
    x_own = jnp.where(s == 0, segment_input[:, 0], out_grad[:, 0]).reshape(rows, feat)
    pool = pool_tokens[:, 0].reshape(-1, enc)
    down = jnp.transpose(enc_down.reshape(peers, head_width, -1), (0, 2, 1))
    down = jnp.pad(down, ((0, 0), (0, -down.shape[1] % 16), (0, 0)))
    wq, wk, wv = w_query[0], w_key[0], w_value[0]

    encoded, x_full, wo_rows = encode(x_own, w_out[0], down, pool, enc_gain[None], enc_up)
    shape_q = ((rows, head_width), BF)
    shape_kv = ((encoded.shape[0], head_width), BF)
    keys, values, queries, probs, part, grad_att = local(
        front_kernel, "front",
        [shape_kv, shape_kv, shape_q, ((tracts, heads, size, slots * NT), F32),
         ((rows, width), BF), shape_q],
        (ids, used, x_full, norm_gain, wq, encoded, wk, wv, wo_rows), 2)
    acts = relay(0, forward_rows, part, (x_full,), 1, peers)
    shape_w = ((enc, head_width), BF)
    accs = [VMEM((head_width, enc), F32)] * 2
    part_back, late_k, late_v = local(
        late_kernel, "late",
        [((rows, width), BF), shape_w, shape_w],
        (ids, used, acts, norm_gain, wq, encoded, keys, values, grad_att), 2,
        [VMEM(*shape_q)] + accs)
    grads = relay(1, backward_rows, part_back, (acts, x_full, norm_gain), 2, peers)
    sum_k, sum_v = local(
        early_kernel, "early",
        [shape_w, shape_w],
        (ids, grads, wo_rows, encoded, values, queries, probs, late_k, late_v), 1,
        [VMEM(*shape_q)] + accs)
    grad_k, grad_v = settle(sum_k, sum_v)
    return (grad_k[None], grad_v[None])


def solution(mesh):
    placed = (
        P(None, "dp", None, "mp"),
        P(None, "dp", None, "mp"),
        P("section", "dp", None, None),
        P(None, "dp", None, None),
        P(None, "dp", None),
        P(),
        P(None, "mp"),
        P(None, "mp"),
        P("section", None),
        P("section", None, "mp"),
        P("section", None, "mp"),
        P("section", None, "mp"),
        P("section", None, "mp"),
    )
    return jax.shard_map(
        on_device,
        mesh=mesh,
        in_specs=placed,
        out_specs=(P("section", None, "mp"), P("section", None, "mp")),
        check_vma=False,
    )
```
